32 devices in a mesh: view: 2 (over x), row: 4 (over z), mat: 4 (over y, core).
Axes of the slice: x: 2, y: 2, z: 4, core: 2. Of those that a mesh axis runs over, the one named last changes fastest.
Arguments:
- volume: float32 [128, 3, 2048], P(('row', 'mat')), may hold values from 0 to 1
- projector: bfloat16 [8, 1024, 2048], P(('view', 'mat')), may hold values from -0.125 to 0.125
- counts: bfloat16 [8, 128, 4, 1024], P(('view', 'mat'), 'row'), may hold values from 0.049804688 to 1
- atten: float32 [4, 3], replicated, may hold values from 0.1 to 1
- newton: bfloat16 [128, 3, 3, 2048], P(('row', 'mat')), may hold values from -0.25 to 0.80078125, as said below
Outputs:
- updated: float32 [128, 3, 2048], P(('row', 'mat'))
The draws below stay inside these ranges and needn't reach their ends.
Inputs may be any that keep to these rules, and one draw needn't show every extreme that they name: newton is symmetric in its two material dimensions; after rounding to bfloat16 its diagonal lies in 0.2 to 0.80078125 and each off-diagonal entry is at most about 0.3 times the root of the two diagonal entries in magnitude.
All inputs are finite; a program needn't handle non-finite values.
Results may differ from the reference program's by a relative error of at most 0.0028.
The reference program's roundings to bfloat16 on the way (of `x_half` and `resid`) count: a program that leaves them out, or rounds other values in their place, can miss the bound.
Values may be sent and summed in bfloat16 or wider, within the bound.
A program may use at most 64 MiB of HBM per device.

```python
import math
import jax
import jax.numpy as jnp
from jax import lax

M = 3
B = 4
U = 1024
PX = 1024
PY = 2
PIX = 2048
VIEWS = 8
Z = 128


def draw_newton(key, part):
    first_key, second_key = jax.random.split(jax.random.fold_in(key, 17))
    diag = jnp.exp(jax.random.uniform(first_key, (Z, M, PIX), jnp.float32, jnp.log(0.2), jnp.log(0.8)))
    couple = jax.random.uniform(second_key, (Z, M, M, PIX), jnp.float32, -1.0, 1.0)
    couple = 0.5 * (couple + jnp.swapaxes(couple, 1, 2))
    root = jnp.sqrt(diag)
    scaled = 0.3 * couple * root[:, :, None, :] * root[:, None, :, :]
    ident = jnp.eye(M, dtype=jnp.float32)[None, :, :, None]
    whole = scaled * (1.0 - ident) + ident * diag[:, :, None, :]
    return whole.astype(jnp.bfloat16)


def level_of(key, extent, cuts, least, high):
    gain = 1.0
    for dim, shards_of in cuts:
        draws = jax.random.uniform(jax.random.fold_in(jax.random.fold_in(key, 6), dim), (shards_of,), jnp.float32, least / len(cuts), high / len(cuts))
        gain = gain * jnp.repeat(jnp.exp(draws), extent[dim] // shards_of).reshape((-1,) + (1,) * (len(extent) - 1 - dim))
    return gain


def gaussian(own_key, dims, scale, limit, shards=(), held_as=jnp.bfloat16):
    result = scale * jax.random.normal(own_key, dims, jnp.float32)
    if shards:
        result = result * level_of(own_key, dims, shards, -0.22, 0.18)
    return jnp.clip(result, -limit, limit).astype(held_as)


def setup_inputs(seed: int = 0) -> dict:
    splits = jax.random.split(jax.random.key(seed), 6)
    volume = jnp.clip(1.0 * jax.random.uniform(splits[0], (Z, M, PIX), jnp.float32) ** level_of(splits[0], (Z, M, PIX), ((0, 16),), -0.2, 0.2), 0.0, 1.0)
    projector = gaussian(splits[1], (VIEWS, U, PIX), PIX ** -0.5, 0.125, ((0, 8),))
    counts = jnp.clip(0.049804688 + 0.9501953 * jax.random.uniform(splits[2], (VIEWS, Z, B, U), jnp.float32) ** level_of(splits[2], (VIEWS, Z, B, U), ((0, 8), (1, 4)), -0.2, 0.2), 0.049804688, 1.0).astype(jnp.bfloat16)
    atten = jnp.clip(jnp.exp(jax.random.uniform(splits[3], (B, M), jnp.float32, math.log(0.1), math.log(1.0))), 0.1, 1.0)
    newton = draw_newton(jax.random.fold_in(splits[5], 71), 0)
    return dict(volume=volume, projector=projector, counts=counts, atten=atten, newton=newton)


HIGH = lax.Precision.HIGHEST

def reference(volume, projector, counts, atten, newton):
    x_half = volume.astype(jnp.bfloat16).astype(jnp.float32)

    def one_view(total, material_pair_index):
        pixel_block_slice, measured_photon_counts = material_pair_index
        blockf = pixel_block_slice.astype(jnp.float32)
        line = jnp.einsum('zmp,up->zmu', x_half, blockf, precision=HIGH)
        expected_counts_model = jnp.exp(-jnp.einsum('bm,zmu->zbu', atten, line, precision=HIGH))
        forward_difference = measured_photon_counts.astype(jnp.float32) - expected_counts_model
        resid = jnp.einsum('bm,zbu->zmu', atten, forward_difference, precision=HIGH)
        resid = resid.astype(jnp.bfloat16).astype(jnp.float32)
        total = total + jnp.einsum('zmu,up->zmp', resid, blockf, precision=HIGH)
        return (total, None)
    start = jnp.zeros((Z, M, PIX), jnp.float32)
    total, unused = lax.scan(one_view, start, (projector, counts))
    grad = total * float(VIEWS) ** (-0.5)
    field = volume.reshape(Z, M, PY, PX)
    pad_z = jnp.pad(field, ((0, 1), (0, 0), (0, 0), (0, 0)))
    pad_y = jnp.pad(field, ((0, 0), (0, 0), (0, 1), (0, 0)))
    pad_x = jnp.pad(field, ((0, 0), (0, 0), (0, 0), (0, 1)))
    diff_z = pad_z[1:] - pad_z[:-1]
    diff_y = pad_y[:, :, 1:] - pad_y[:, :, :-1]
    diff_x = pad_x[:, :, :, 1:] - pad_x[:, :, :, :-1]
    scale = jnp.sqrt(0.25 + lax.optimization_barrier(jnp.sum(diff_z * diff_z + diff_y * diff_y + diff_x * diff_x, axis=1, keepdims=True)))
    flux_z = diff_z / scale
    flux_y = diff_y / scale
    flux_x = diff_x / scale
    prev_z = jnp.pad(flux_z, ((1, 0), (0, 0), (0, 0), (0, 0)))[:-1]
    prev_y = jnp.pad(flux_y, ((0, 0), (0, 0), (1, 0), (0, 0)))[:, :, :-1]
    prev_x = jnp.pad(flux_x, ((0, 0), (0, 0), (0, 0), (1, 0)))[:, :, :, :-1]
    smooth = prev_z - flux_z + (prev_y - flux_y) + (prev_x - flux_x)
    smooth = smooth.reshape(Z, M, PIX)
    step_dir = grad + 0.5 * smooth
    hess = newton.astype(jnp.float32)
    return volume - lax.optimization_barrier(jnp.sum(hess * step_dir[:, None], axis=2))
```

```python
import functools

import jax
import jax.numpy as jnp
from jax import lax
from jax.experimental import pallas as pl
from jax.experimental.pallas import tpu as pltpu
from jax.sharding import PartitionSpec as P

PX = 1024
CHUNKS = 4
MESH = pl.DeviceIdType.MESH
F32 = jnp.float32
BF16 = jnp.bfloat16


def shift_rows(field, by):
    zero = jnp.zeros((field.shape[0], PX), F32)
    if by > 0:
        return jnp.concatenate([zero, field[:, :-PX]], 1)
    return jnp.concatenate([field[:, PX:], zero], 1)


def shift_pix(field, by):
    size = field.shape[1]
    column = lax.broadcasted_iota(jnp.int32, field.shape, 1) % PX
    rolled = pltpu.roll(field, by % size, 1)
    edge = 0 if by > 0 else PX - 1
    return jnp.where(column == edge, 0.0, rolled)


def kernel(dims, vol_hbm, vt_hbm, proj_hbm, cnt_hbm, nw_hbm, atten, out,
           vt, proj, cnt, nw, halo, xs, acc, res, base, g0, s1, r1, s2, r2, r3,
           loc_sem, proj_sem, halo_s, halo_r, agp_s, agp_r, agy_s, agy_r, agf_s, agf_r,
           rs1_s, rs1_r, rs2_s, rs2_r, rs3_s, rs3_r):
    views, rows, mats, mat_count, bins, depth, width, views_all = dims
    half = mats // 2
    v, r, i = lax.axis_index("view"), lax.axis_index("row"), lax.axis_index("mat")
    par = i % 2
    group = i // 2
    pair = (v, r, i + 1 - 2 * par)
    peers = [None] + [(v, r, 2 * lax.rem(group + d, half) + par) for d in range(1, half)]
    others = [None] + [(lax.rem(v + d, views), r, i) for d in range(1, views)]
    slab = r * mats + i
    slabs = rows * mats
    up, down = lax.rem(slab + 1, slabs), lax.rem(slab + slabs - 1, slabs)
    above = (v, up // mats, up % mats)
    below = (v, down // mats, down % mats)

    barrier = pltpu.get_barrier_semaphore()
    greet = [pair, above, below] + peers[1:] + others[1:]
    for device in greet:
        pl.semaphore_signal(barrier, inc=1, device_id=device, device_id_type=MESH)

    load_vol = pltpu.make_async_copy(vt_hbm, vt, loc_sem.at[0])
    load_vol.start()
    load_proj = []
    for c in range(CHUNKS):
        cols = pl.ds(c * width, width)
        load_proj.append(pltpu.make_async_copy(proj_hbm.at[0, :, cols], proj.at[:, cols], proj_sem.at[c]))
        load_proj[c].start()
    load_cnt = pltpu.make_async_copy(cnt_hbm, cnt, loc_sem.at[1])
    load_cnt.start()
    load_nw = pltpu.make_async_copy(nw_hbm, nw, loc_sem.at[2])
    load_nw.start()

    load_vol.wait()
    for c in range(CHUNKS):
        cols = slice(c * width, (c + 1) * width)
        xs[c, 0] = jnp.concatenate([vt[m, :, cols] for m in range(mat_count)], 0).astype(BF16)
    pl.semaphore_wait(barrier, len(greet))

    def send(src, dst, s, t, device):
        copy = pltpu.make_async_remote_copy(src, dst, s, t, device_id=device, device_id_type=MESH)
        copy.start()
        return copy

    agy = [[None] * half for c in range(CHUNKS)]
    agp = []
    for c in range(CHUNKS):
        for d in range(1, half):
            agy[c][d] = send(xs.at[c, 0], xs.at[c, 2 * (half - d)], agy_s.at[c, d - 1],
                             agy_r.at[c, half - d - 1], peers[d])
        agp.append(send(xs.at[c, 0], xs.at[c, 1], agp_s.at[c], agp_r.at[c], pair))
    to_below = send(vol_hbm.at[0], halo.at[0], halo_s.at[0], halo_r.at[0], below)
    to_above = send(vol_hbm.at[depth - 1], halo.at[1], halo_s.at[1], halo_r.at[1], above)

    to_below.wait_recv()
    to_above.wait_recv()
    load_nw.wait()
    z = lax.broadcasted_iota(jnp.int32, vt.shape[1:], 0)
    last, first = slab == slabs - 1, slab == 0
    cur = [vt[m] for m in range(mat_count)]
    after = [jnp.where(z == depth - 1, jnp.where(last, 0.0, halo[0, m:m + 1, :]), pltpu.roll(cur[m], depth - 1, 0))
             for m in range(mat_count)]
    before = [jnp.where(z == 0, halo[1, m:m + 1, :], pltpu.roll(cur[m], 1, 0)) for m in range(mat_count)]

    def fluxes(lower, upper):
        dz = [b - a for a, b in zip(lower, upper)]
        dy = [shift_rows(a, -1) - a for a in lower]
        dx = [shift_pix(a, -1) - a for a in lower]
        total = 0.25
        for m in range(mat_count):
            total = total + (dz[m] * dz[m] + dy[m] * dy[m] + dx[m] * dx[m])
        scale = 1.0 / jnp.sqrt(total)
        return [a * scale for a in dz], [a * scale for a in dy], [a * scale for a in dx]

    qz, qy, qx = fluxes(cur, after)
    pz, _, _ = fluxes(before, cur)
    tv = []
    for m in range(mat_count):
        prev_z = jnp.where(jnp.logical_and(first, z == 0), 0.0, pz[m])
        tv.append(0.5 * ((prev_z - qz[m]) + (shift_rows(qy[m], 1) - qy[m]) + (shift_pix(qx[m], 1) - qx[m])))
    for m in range(mat_count):
        total = nw[m, 0].astype(F32) * tv[0]
        for k in range(1, mat_count):
            total = total + nw[m, k].astype(F32) * tv[k]
        base[m] = cur[m] - total

    agf = [[None] * half for c in range(CHUNKS)]
    for c in range(CHUNKS):
        for d in range(1, half):
            agy[c][half - d].wait_recv()
            agf[c][d] = send(xs.at[c, 2 * d], xs.at[c, 2 * d + 1], agf_s.at[c, d - 1], agf_r.at[c, d - 1], pair)
    for c in range(CHUNKS):
        load_proj[c].wait()
        agp[c].wait_recv()
        for d in range(1, half):
            agf[c][d].wait_recv()
        x = jnp.concatenate([xs[c, s] for s in range(mats)], 0)
        part = lax.dot_general(x, proj[:, c * width:(c + 1) * width], (((1,), (1,)), ((), ())),
                               preferred_element_type=F32)
        if c == 0:
            acc[...] = part
        else:
            acc[...] += part

    load_cnt.wait()
    span = mat_count * depth
    for s in range(mats):
        owner = 2 * lax.rem(group + s // 2, half) + (par if s % 2 == 0 else 1 - par)
        line = [acc[s * span + m * depth:s * span + (m + 1) * depth, :] for m in range(mat_count)]
        parts = [None] * mat_count
        for b in range(bins):
            expo = atten[b, 0] * line[0]
            for m in range(1, mat_count):
                expo = expo + atten[b, m] * line[m]
            diff = cnt[owner, b].astype(F32) - jnp.exp(-expo)
            for m in range(mat_count):
                term = atten[b, m] * diff
                parts[m] = term if parts[m] is None else parts[m] + term
        res[s] = jnp.concatenate(parts, 0).astype(BF16)

    rs1 = []
    resid = jnp.concatenate([res[s] for s in range(mats)], 0)
    for c in range(CHUNKS):
        part = jnp.dot(resid, proj[:, c * width:(c + 1) * width], preferred_element_type=F32)
        for d in range(half):
            s1[c, d] = part[(2 * d + 1) * span:(2 * d + 2) * span].astype(BF16)
            g0[c, d] = part[2 * d * span:(2 * d + 1) * span]
        rs1.append(send(s1.at[c], r1.at[c], rs1_s.at[c], rs1_r.at[c], pair))
    rs2 = [[None] * half for c in range(CHUNKS)]
    for c in range(CHUNKS):
        rs1[c].wait_recv()
        for d in range(1, half):
            s2[c, d - 1] = (g0[c, d] + r1[c, d].astype(F32)).astype(BF16)
            rs2[c][d] = send(s2.at[c, d - 1], r2.at[c, half - d - 1], rs2_s.at[c, d - 1],
                             rs2_r.at[c, half - d - 1], peers[d])
        g0[c, 0] = g0[c, 0] + r1[c, 0].astype(F32)
    rs3 = [[None] * views for c in range(CHUNKS)]
    for c in range(CHUNKS):
        total = g0[c, 0]
        for d in range(1, half):
            rs2[c][half - d].wait_recv()
            total = total + r2[c, d - 1].astype(F32)
        r3[c, v] = total.astype(BF16)
        for d in range(1, views):
            rs3[c][d] = send(r3.at[c, v], r3.at[c, v], rs3_s.at[c, d - 1], rs3_r.at[c, views - d - 1], others[d])
    for c in range(CHUNKS):
        cols = slice(c * width, (c + 1) * width)
        for d in range(1, views):
            source = lax.rem(v + views - d, views)
            pltpu.make_async_remote_copy(r3.at[c, source], r3.at[c, source], rs3_s.at[c, d - 1],
                                         rs3_r.at[c, views - d - 1], device_id=others[d],
                                         device_id_type=MESH).wait_recv()
        grad = r3[c, 0].astype(F32)
        for w in range(1, views):
            grad = grad + r3[c, w].astype(F32)
        grad = grad * float(views_all) ** (-0.5)
        for m in range(mat_count):
            total = nw[m, 0, :, cols].astype(F32) * grad[:depth]
            for k in range(1, mat_count):
                total = total + nw[m, k, :, cols].astype(F32) * grad[k * depth:(k + 1) * depth]
            out[m, :, cols] = base[m, :, cols] - total

    to_below.wait_send()
    to_above.wait_send()
    for c in range(CHUNKS):
        agp[c].wait_send()
        rs1[c].wait_send()
        for d in range(1, half):
            agy[c][d].wait_send()
            agf[c][d].wait_send()
            rs2[c][d].wait_send()
        for d in range(1, views):
            rs3[c][d].wait_send()


def body(volume, projector, counts, atten, newton):
    views, rows, mats = (lax.axis_size(a) for a in ("view", "row", "mat"))
    depth, mat_count, pixels = volume.shape
    columns = projector.shape[1]
    bins = atten.shape[0]
    views_all = projector.shape[0] * views * mats
    width = pixels // CHUNKS
    half = mats // 2
    span = depth * mat_count
    vol_t = jnp.transpose(volume, (1, 0, 2))
    cnt_t = jnp.transpose(counts.reshape(mats, depth, bins, columns), (0, 2, 1, 3))
    nw_t = jnp.transpose(newton, (1, 2, 0, 3))
    dims = (views, rows, mats, mat_count, bins, depth, width, views_all)
    any_spec = pl.BlockSpec(memory_space=pl.ANY)
    dma = pltpu.SemaphoreType.DMA
    out = pl.pallas_call(
        functools.partial(kernel, dims),
        out_shape=jax.ShapeDtypeStruct((mat_count, depth, pixels), F32),
        in_specs=[any_spec] * 5 + [pl.BlockSpec(memory_space=pltpu.SMEM)],
        out_specs=pl.BlockSpec(memory_space=pltpu.VMEM),
        scratch_shapes=[
            pltpu.VMEM((mat_count, depth, pixels), F32),
            pltpu.VMEM((columns, pixels), BF16),
            pltpu.VMEM((mats, bins, depth, columns), BF16),
            pltpu.VMEM((mat_count, mat_count, depth, pixels), BF16),
            pltpu.VMEM((2, mat_count, pixels), F32),
            pltpu.VMEM((CHUNKS, mats, span, width), BF16),
            pltpu.VMEM((mats * span, columns), F32),
            pltpu.VMEM((mats, span, columns), BF16),
            pltpu.VMEM((mat_count, depth, pixels), F32),
            pltpu.VMEM((CHUNKS, half, span, width), F32),
            pltpu.VMEM((CHUNKS, half, span, width), BF16),
            pltpu.VMEM((CHUNKS, half, span, width), BF16),
            pltpu.VMEM((CHUNKS, half - 1, span, width), BF16),
            pltpu.VMEM((CHUNKS, half - 1, span, width), BF16),
            pltpu.VMEM((CHUNKS, views, span, width), BF16),
            dma((3,)), dma((CHUNKS,)), dma((2,)), dma((2,)),
            dma((CHUNKS,)), dma((CHUNKS,)),
            dma((CHUNKS, half - 1)), dma((CHUNKS, half - 1)),
            dma((CHUNKS, half - 1)), dma((CHUNKS, half - 1)),
            dma((CHUNKS,)), dma((CHUNKS,)),
            dma((CHUNKS, half - 1)), dma((CHUNKS, half - 1)),
            dma((CHUNKS, views - 1)), dma((CHUNKS, views - 1)),
        ],
        compiler_params=pltpu.CompilerParams(
            collective_id=0, has_side_effects=True, vmem_limit_bytes=48 * 1024 * 1024
        ),
    )(volume, vol_t, projector, cnt_t, nw_t, atten)
    return jnp.transpose(out, (1, 0, 2))


def solution(mesh):
    in_specs = (
        P(("row", "mat"), None, None),
        P(("view", "mat"), None, None),
        P(("view", "mat"), "row", None, None),
        P(),
        P(("row", "mat"), None, None, None),
    )
    out_specs = P(("row", "mat"), None, None)
    return jax.shard_map(body, mesh=mesh, in_specs=in_specs, out_specs=out_specs, check_vma=False)
```

```python
import functools

import jax
import jax.numpy as jnp
from jax import lax
from jax.experimental import pallas as pl
from jax.experimental.pallas import tpu as pltpu
from jax.sharding import PartitionSpec as P

PX = 1024
CHUNKS = 4
MESH = pl.DeviceIdType.MESH
F32 = jnp.float32
BF16 = jnp.bfloat16


def shift_rows(field, by):
    zero = jnp.zeros((field.shape[0], PX), F32)
    if by > 0:
        return jnp.concatenate([zero, field[:, :-PX]], 1)
    return jnp.concatenate([field[:, PX:], zero], 1)


def shift_pix(field, by):
    size = field.shape[1]
    column = lax.broadcasted_iota(jnp.int32, field.shape, 1) % PX
    rolled = pltpu.roll(field, by % size, 1)
    edge = 0 if by > 0 else PX - 1
    return jnp.where(column == edge, 0.0, rolled)


def kernel(dims, vt_hbm, proj_hbm, cnt_hbm, nw_hbm, atten_hbm, out,
           vt, proj, cnt_in, cnt, nw, atten, edge, halo, xs, acc, res, base, g0, s1, r1, s2, r2, r3,
           loc_sem, proj_sem, halo_s, halo_r, agp_s, agp_r, agy_s, agy_r, agf_s, agf_r,
           rs1_s, rs1_r, rs2_s, rs2_r, rs3_s, rs3_r):
    views, rows, mats, mat_count, bins, depth, width, views_all = dims
    half = mats // 2
    v, r, i = lax.axis_index("view"), lax.axis_index("row"), lax.axis_index("mat")
    par = i % 2
    group = i // 2
    pair = (v, r, i + 1 - 2 * par)
    peers = [None] + [(v, r, 2 * lax.rem(group + d, half) + par) for d in range(1, half)]
    others = [None] + [(lax.rem(v + d, views), r, i) for d in range(1, views)]
    slab = r * mats + i
    slabs = rows * mats
    up, down = lax.rem(slab + 1, slabs), lax.rem(slab + slabs - 1, slabs)
    above = (v, up // mats, up % mats)
    below = (v, down // mats, down % mats)

    barrier = pltpu.get_barrier_semaphore()
    greet = [pair, above, below] + peers[1:] + others[1:]
    for device in greet:
        pl.semaphore_signal(barrier, inc=1, device_id=device, device_id_type=MESH)

    load_vol = pltpu.make_async_copy(vt_hbm, vt, loc_sem.at[0])
    load_vol.start()
    load_proj = []
    for c in range(CHUNKS):
        cols = pl.ds(c * width, width)
        load_proj.append(pltpu.make_async_copy(proj_hbm.at[0, :, cols], proj.at[:, cols], proj_sem.at[c]))
        load_proj[c].start()
    load_cnt = pltpu.make_async_copy(cnt_hbm, cnt_in, loc_sem.at[1])
    load_att = pltpu.make_async_copy(atten_hbm, atten, loc_sem.at[3])
    load_att.start()
    load_cnt.start()
    load_nw = pltpu.make_async_copy(nw_hbm, nw, loc_sem.at[2])
    load_nw.start()

    load_vol.wait()
    edge[0] = jnp.concatenate([vt[m, 0:1, :] for m in range(mat_count)], 0)
    edge[1] = jnp.concatenate([vt[m, depth - 1:depth, :] for m in range(mat_count)], 0)
    for c in range(CHUNKS):
        cols = slice(c * width, (c + 1) * width)
        xs[c, 0] = jnp.concatenate([vt[m, :, cols] for m in range(mat_count)], 0).astype(BF16)
    pl.semaphore_wait(barrier, len(greet))

    def send(src, dst, s, t, device):
        copy = pltpu.make_async_remote_copy(src, dst, s, t, device_id=device, device_id_type=MESH)
        copy.start()
        return copy

    agy = [[None] * half for c in range(CHUNKS)]
    agp = []
    for c in range(CHUNKS):
        for d in range(1, half):
            agy[c][d] = send(xs.at[c, 0], xs.at[c, 2 * (half - d)], agy_s.at[c, d - 1],
                             agy_r.at[c, half - d - 1], peers[d])
        agp.append(send(xs.at[c, 0], xs.at[c, 1], agp_s.at[c], agp_r.at[c], pair))
    to_below = send(edge.at[0], halo.at[0], halo_s.at[0], halo_r.at[0], below)
    to_above = send(edge.at[1], halo.at[1], halo_s.at[1], halo_r.at[1], above)

    to_below.wait_recv()
    to_above.wait_recv()
    load_nw.wait()
    z = lax.broadcasted_iota(jnp.int32, vt.shape[1:], 0)
    last, first = slab == slabs - 1, slab == 0
    cur = [vt[m] for m in range(mat_count)]
    after = [jnp.where(z == depth - 1, jnp.where(last, 0.0, halo[0, m:m + 1, :]), pltpu.roll(cur[m], depth - 1, 0))
             for m in range(mat_count)]
    before = [jnp.where(z == 0, halo[1, m:m + 1, :], pltpu.roll(cur[m], 1, 0)) for m in range(mat_count)]

    def fluxes(lower, upper):
        dz = [b - a for a, b in zip(lower, upper)]
        dy = [shift_rows(a, -1) - a for a in lower]
        dx = [shift_pix(a, -1) - a for a in lower]
        total = 0.25
        for m in range(mat_count):
            total = total + (dz[m] * dz[m] + dy[m] * dy[m] + dx[m] * dx[m])
        scale = 1.0 / jnp.sqrt(total)
        return [a * scale for a in dz], [a * scale for a in dy], [a * scale for a in dx]

    qz, qy, qx = fluxes(cur, after)
    pz, _, _ = fluxes(before, cur)
    tv = []
    for m in range(mat_count):
        prev_z = jnp.where(jnp.logical_and(first, z == 0), 0.0, pz[m])
        tv.append(0.5 * ((prev_z - qz[m]) + (shift_rows(qy[m], 1) - qy[m]) + (shift_pix(qx[m], 1) - qx[m])))
    for m in range(mat_count):
        total = nw[m, 0].astype(F32) * tv[0]
        for k in range(1, mat_count):
            total = total + nw[m, k].astype(F32) * tv[k]
        base[m] = cur[m] - total

    load_att.wait()
    load_cnt.wait()
    for j in range(mats):
        tiles = [cnt_in[j, a].astype(F32) for a in range(depth)]
        for b in range(bins):
            cnt[j, b] = jnp.concatenate([tile[b:b + 1] for tile in tiles], 0)

    agf = [[None] * half for c in range(CHUNKS)]
    for c in range(CHUNKS):
        for d in range(1, half):
            agy[c][half - d].wait_recv()
            agf[c][d] = send(xs.at[c, 2 * d], xs.at[c, 2 * d + 1], agf_s.at[c, d - 1], agf_r.at[c, d - 1], pair)
    for c in range(CHUNKS):
        load_proj[c].wait()
        agp[c].wait_recv()
        for d in range(1, half):
            agf[c][d].wait_recv()
        x = jnp.concatenate([xs[c, s] for s in range(mats)], 0)
        part = lax.dot_general(x, proj[:, c * width:(c + 1) * width], (((1,), (1,)), ((), ())),
                               preferred_element_type=F32)
        if c == 0:
            acc[...] = part
        else:
            acc[...] += part

    span = mat_count * depth
    for s in range(mats):
        owner = 2 * lax.rem(group + s // 2, half) + (par if s % 2 == 0 else 1 - par)
        line = [acc[s * span + m * depth:s * span + (m + 1) * depth, :] for m in range(mat_count)]
        parts = [None] * mat_count
        for b in range(bins):
            expo = atten[b, 0] * line[0]
            for m in range(1, mat_count):
                expo = expo + atten[b, m] * line[m]
            diff = cnt[owner, b] - jnp.exp(-expo)
            for m in range(mat_count):
                term = atten[b, m] * diff
                parts[m] = term if parts[m] is None else parts[m] + term
        res[s] = jnp.concatenate(parts, 0).astype(BF16)

    rs1 = []
    resid = jnp.concatenate([res[s] for s in range(mats)], 0)
    for c in range(CHUNKS):
        part = jnp.dot(resid, proj[:, c * width:(c + 1) * width], preferred_element_type=F32)
        for d in range(half):
            s1[c, d] = part[(2 * d + 1) * span:(2 * d + 2) * span].astype(BF16)
            g0[c, d] = part[2 * d * span:(2 * d + 1) * span]
        rs1.append(send(s1.at[c], r1.at[c], rs1_s.at[c], rs1_r.at[c], pair))
    rs2 = [[None] * half for c in range(CHUNKS)]
    for c in range(CHUNKS):
        rs1[c].wait_recv()
        for d in range(1, half):
            s2[c, d - 1] = (g0[c, d] + r1[c, d].astype(F32)).astype(BF16)
            rs2[c][d] = send(s2.at[c, d - 1], r2.at[c, half - d - 1], rs2_s.at[c, d - 1],
                             rs2_r.at[c, half - d - 1], peers[d])
        g0[c, 0] = g0[c, 0] + r1[c, 0].astype(F32)
    rs3 = [[None] * views for c in range(CHUNKS)]
    for c in range(CHUNKS):
        total = g0[c, 0]
        for d in range(1, half):
            rs2[c][half - d].wait_recv()
            total = total + r2[c, d - 1].astype(F32)
        r3[c, v] = total.astype(BF16)
        for d in range(1, views):
            rs3[c][d] = send(r3.at[c, v], r3.at[c, v], rs3_s.at[c, d - 1], rs3_r.at[c, views - d - 1], others[d])
    for c in range(CHUNKS):
        cols = slice(c * width, (c + 1) * width)
        for d in range(1, views):
            source = lax.rem(v + views - d, views)
            pltpu.make_async_remote_copy(r3.at[c, source], r3.at[c, source], rs3_s.at[c, d - 1],
                                         rs3_r.at[c, views - d - 1], device_id=others[d],
                                         device_id_type=MESH).wait_recv()
        grad = r3[c, 0].astype(F32)
        for w in range(1, views):
            grad = grad + r3[c, w].astype(F32)
        grad = grad * float(views_all) ** (-0.5)
        for m in range(mat_count):
            total = nw[m, 0, :, cols].astype(F32) * grad[:depth]
            for k in range(1, mat_count):
                total = total + nw[m, k, :, cols].astype(F32) * grad[k * depth:(k + 1) * depth]
            out[m, :, cols] = base[m, :, cols] - total

    to_below.wait_send()
    to_above.wait_send()
    for c in range(CHUNKS):
        agp[c].wait_send()
        rs1[c].wait_send()
        for d in range(1, half):
            agy[c][d].wait_send()
            agf[c][d].wait_send()
            rs2[c][d].wait_send()
        for d in range(1, views):
            rs3[c][d].wait_send()


def body(volume, projector, counts, atten, newton):
    views, rows, mats = (lax.axis_size(a) for a in ("view", "row", "mat"))
    depth, mat_count, pixels = volume.shape
    columns = projector.shape[1]
    bins = atten.shape[0]
    views_all = projector.shape[0] * views * mats
    width = pixels // CHUNKS
    half = mats // 2
    span = depth * mat_count
    vol_t = jnp.transpose(volume, (1, 0, 2))
    cnt = counts.reshape(mats, depth, bins, columns)
    nw_t = jnp.transpose(newton, (1, 2, 0, 3))
    dims = (views, rows, mats, mat_count, bins, depth, width, views_all)
    hbm = pl.BlockSpec(memory_space=pltpu.HBM)
    dma = pltpu.SemaphoreType.DMA
    out = pl.pallas_call(
        functools.partial(kernel, dims),
        out_shape=jax.ShapeDtypeStruct((mat_count, depth, pixels), F32),
        in_specs=[hbm] * 5,
        out_specs=pl.BlockSpec(memory_space=pltpu.VMEM),
        scratch_shapes=[
            pltpu.VMEM((mat_count, depth, pixels), F32),
            pltpu.VMEM((columns, pixels), BF16),
            pltpu.VMEM((mats, depth, bins, columns), BF16),
            pltpu.VMEM((mats, bins, depth, columns), F32),
            pltpu.VMEM((mat_count, mat_count, depth, pixels), BF16),
            pltpu.SMEM(atten.shape, F32),
            pltpu.VMEM((2, mat_count, pixels), F32),
            pltpu.VMEM((2, mat_count, pixels), F32),
            pltpu.VMEM((CHUNKS, mats, span, width), BF16),
            pltpu.VMEM((mats * span, columns), F32),
            pltpu.VMEM((mats, span, columns), BF16),
            pltpu.VMEM((mat_count, depth, pixels), F32),
            pltpu.VMEM((CHUNKS, half, span, width), F32),
            pltpu.VMEM((CHUNKS, half, span, width), BF16),
            pltpu.VMEM((CHUNKS, half, span, width), BF16),
            pltpu.VMEM((CHUNKS, half - 1, span, width), BF16),
            pltpu.VMEM((CHUNKS, half - 1, span, width), BF16),
            pltpu.VMEM((CHUNKS, views, span, width), BF16),
            dma((4,)), dma((CHUNKS,)), dma((2,)), dma((2,)),
            dma((CHUNKS,)), dma((CHUNKS,)),
            dma((CHUNKS, half - 1)), dma((CHUNKS, half - 1)),
            dma((CHUNKS, half - 1)), dma((CHUNKS, half - 1)),
            dma((CHUNKS,)), dma((CHUNKS,)),
            dma((CHUNKS, half - 1)), dma((CHUNKS, half - 1)),
            dma((CHUNKS, views - 1)), dma((CHUNKS, views - 1)),
        ],
        compiler_params=pltpu.CompilerParams(
            collective_id=0, has_side_effects=True, vmem_limit_bytes=67043328
        ),
    )(vol_t, projector, cnt, nw_t, atten)
    return jnp.transpose(out, (1, 0, 2))


def solution(mesh):
    in_specs = (
        P(("row", "mat"), None, None),
        P(("view", "mat"), None, None),
        P(("view", "mat"), "row", None, None),
        P(),
        P(("row", "mat"), None, None, None),
    )
    out_specs = P(("row", "mat"), None, None)
    return jax.shard_map(body, mesh=mesh, in_specs=in_specs, out_specs=out_specs, check_vma=False)
```

```python
import functools

import jax
import jax.numpy as jnp
from jax import lax
from jax.experimental import pallas as pl
from jax.experimental.pallas import tpu as pltpu
from jax.sharding import PartitionSpec as P

PX = 1024
CHUNKS = 8
ROOM = 208 * 1024
MESH = pl.DeviceIdType.MESH
F32 = jnp.float32
BF16 = jnp.bfloat16


def shift_rows(field, by):
    zero = jnp.zeros((field.shape[0], PX), F32)
    if by > 0:
        return jnp.concatenate([zero, field[:, :-PX]], 1)
    return jnp.concatenate([field[:, PX:], zero], 1)


def shift_pix(field, by):
    size = field.shape[1]
    column = lax.broadcasted_iota(jnp.int32, field.shape, 1) % PX
    rolled = pltpu.roll(field, by % size, 1)
    edge = 0 if by > 0 else PX - 1
    return jnp.where(column == edge, 0.0, rolled)


def kernel(dims, vt_hbm, proj_hbm, cnt_hbm, nw_hbm, atten_hbm, out,
           vt, proj, cnt_in, cnt, nw, atten, edge, halo, xs, acc, res, base, g0, s1, r1, s2, r2, r3,
           loc_sem, vol_sem, proj_sem, halo_s, halo_r, agp_s, agp_r, agy_s, agy_r, agf_s, agf_r,
           rs1_s, rs1_r, rs2_s, rs2_r, rs3_s, rs3_r):
    views, rows, mats, mat_count, bins, depth, width, views_all = dims
    half = mats // 2
    v, r, i = lax.axis_index("view"), lax.axis_index("row"), lax.axis_index("mat")
    par = i % 2
    group = i // 2
    pair = (v, r, i + 1 - 2 * par)
    peers = [None] + [(v, r, 2 * lax.rem(group + d, half) + par) for d in range(1, half)]
    others = [None] + [(lax.rem(v + d, views), r, i) for d in range(1, views)]
    slab = r * mats + i
    slabs = rows * mats
    up, down = lax.rem(slab + 1, slabs), lax.rem(slab + slabs - 1, slabs)
    above = (v, up // mats, up % mats)
    below = (v, down // mats, down % mats)

    barrier = pltpu.get_barrier_semaphore()
    last, first = slab == slabs - 1, slab == 0
    greet = [pair] + peers[1:] + others[1:]
    for device in greet:
        pl.semaphore_signal(barrier, inc=1, device_id=device, device_id_type=MESH)

    @pl.when(jnp.logical_not(first))
    def _():
        pl.semaphore_signal(barrier, inc=1, device_id=below, device_id_type=MESH)

    @pl.when(jnp.logical_not(last))
    def _():
        pl.semaphore_signal(barrier, inc=1, device_id=above, device_id_type=MESH)

    load_vol = []
    for c in range(CHUNKS):
        cols = pl.ds(c * width, width)
        load_vol.append(pltpu.make_async_copy(vt_hbm.at[:, :, cols], vt.at[:, :, cols], vol_sem.at[c]))
        load_vol[c].start()
    load_proj = []
    for c in range(CHUNKS):
        cols = pl.ds(c * width, width)
        load_proj.append(pltpu.make_async_copy(proj_hbm.at[0, :, cols], proj.at[:, cols], proj_sem.at[c]))
        load_proj[c].start()
    load_cnt = pltpu.make_async_copy(cnt_hbm, cnt_in, loc_sem.at[1])
    load_att = pltpu.make_async_copy(atten_hbm, atten, loc_sem.at[3])
    load_att.start()
    load_cnt.start()
    load_nw = pltpu.make_async_copy(nw_hbm, nw, loc_sem.at[2])
    load_nw.start()

    def send(src, dst, s, t, device):
        copy = pltpu.make_async_remote_copy(src, dst, s, t, device_id=device, device_id_type=MESH)
        copy.start()
        return copy

    def halo_copy(way, device):
        return pltpu.make_async_remote_copy(edge.at[way], halo.at[way], halo_s.at[way], halo_r.at[way],
                                            device_id=device, device_id_type=MESH)

    to_below, to_above = halo_copy(0, below), halo_copy(1, above)
    agy = [[None] * half for c in range(CHUNKS)]
    agp = []
    for c in range(CHUNKS):
        cols = slice(c * width, (c + 1) * width)
        if c == 0:
            load_vol[c].wait()
        xs[c, 0] = jnp.concatenate([vt[m, :, cols] for m in range(mat_count)], 0).astype(BF16)
        if c == 0:
            ends = jnp.where(first, 1, 0) + jnp.where(last, 1, 0)
            pl.semaphore_wait(barrier, len(greet) + 2 - ends)
        for d in range(1, half):
            agy[c][d] = send(xs.at[c, 0], xs.at[c, 2 * (half - d)], agy_s.at[c, d - 1],
                             agy_r.at[c, half - d - 1], peers[d])
        agp.append(send(xs.at[c, 0], xs.at[c, 1], agp_s.at[c], agp_r.at[c], pair))
        if c == 0:
            for rest in load_vol[1:]:
                rest.wait()
            edge[0] = jnp.concatenate([vt[m, 0:1, :] for m in range(mat_count)], 0)
            edge[1] = jnp.concatenate([vt[m, depth - 1:depth, :] for m in range(mat_count)], 0)

            @pl.when(jnp.logical_not(first))
            def _():
                to_below.start()

            @pl.when(jnp.logical_not(last))
            def _():
                to_above.start()

    load_att.wait()
    load_cnt.wait()
    for j in range(mats):
        tiles = [cnt_in[j, a].astype(F32) for a in range(depth)]
        for b in range(bins):
            cnt[j, b] = jnp.concatenate([tile[b:b + 1] for tile in tiles], 0)

    def regularise():
        @pl.when(jnp.logical_not(last))
        def _():
            to_below.wait_recv()

        @pl.when(last)
        def _():
            halo[0] = jnp.zeros(halo.shape[1:], F32)

        @pl.when(jnp.logical_not(first))
        def _():
            to_above.wait_recv()

        @pl.when(first)
        def _():
            halo[1] = jnp.zeros(halo.shape[1:], F32)

        load_nw.wait()
        z = lax.broadcasted_iota(jnp.int32, vt.shape[1:], 0)
        cur = [vt[m] for m in range(mat_count)]
        after = [jnp.where(z == depth - 1, halo[0, m:m + 1, :], pltpu.roll(cur[m], depth - 1, 0))
                 for m in range(mat_count)]
        before = [jnp.where(z == 0, halo[1, m:m + 1, :], pltpu.roll(cur[m], 1, 0)) for m in range(mat_count)]

        def fluxes(lower, upper):
            dz = [b - a for a, b in zip(lower, upper)]
            dy = [shift_rows(a, -1) - a for a in lower]
            dx = [shift_pix(a, -1) - a for a in lower]
            total = 0.25
            for m in range(mat_count):
                total = total + (dz[m] * dz[m] + dy[m] * dy[m] + dx[m] * dx[m])
            scale = 1.0 / jnp.sqrt(total)
            return [a * scale for a in dz], [a * scale for a in dy], [a * scale for a in dx]

        qz, qy, qx = fluxes(cur, after)
        pz, _, _ = fluxes(before, cur)
        tv = []
        for m in range(mat_count):
            prev_z = jnp.where(jnp.logical_and(first, z == 0), 0.0, pz[m])
            tv.append(0.5 * ((prev_z - qz[m]) + (shift_rows(qy[m], 1) - qy[m]) + (shift_pix(qx[m], 1) - qx[m])))
        for m in range(mat_count):
            total = nw[m, 0].astype(F32) * tv[0]
            for k in range(1, mat_count):
                total = total + nw[m, k].astype(F32) * tv[k]
            base[m] = cur[m] - total

    agf = [[None] * half for c in range(CHUNKS)]

    def relay(c):
        for d in range(1, half):
            agy[c][half - d].wait_recv()
            agf[c][d] = send(xs.at[c, 2 * d], xs.at[c, 2 * d + 1], agf_s.at[c, d - 1], agf_r.at[c, d - 1], pair)

    def forward(c):
        load_proj[c].wait()
        agp[c].wait_recv()
        for d in range(1, half):
            agf[c][d].wait_recv()
        x = jnp.concatenate([xs[c, s] for s in range(mats)], 0)
        part = lax.dot_general(x, proj[:, c * width:(c + 1) * width], (((1,), (1,)), ((), ())),
                               preferred_element_type=F32)
        if c == 0:
            acc[...] = part
        else:
            acc[...] += part

    lag = CHUNKS // 2
    for c in range(CHUNKS):
        relay(c)
        if c == 0:
            regularise()
        if c >= lag:
            forward(c - lag)
    for c in range(CHUNKS - lag, CHUNKS):
        forward(c)

    span = mat_count * depth
    for s in range(mats):
        owner = 2 * lax.rem(group + s // 2, half) + (par if s % 2 == 0 else 1 - par)
        line = [acc[s * span + m * depth:s * span + (m + 1) * depth, :] for m in range(mat_count)]
        parts = [None] * mat_count
        for b in range(bins):
            expo = atten[b, 0] * line[0]
            for m in range(1, mat_count):
                expo = expo + atten[b, m] * line[m]
            diff = cnt[owner, b] - jnp.exp(-expo)
            for m in range(mat_count):
                term = atten[b, m] * diff
                parts[m] = term if parts[m] is None else parts[m] + term
        res[s] = jnp.concatenate(parts, 0).astype(BF16)

    rs1 = []
    resid = jnp.concatenate([res[s] for s in range(mats)], 0)
    for c in range(CHUNKS):
        part = jnp.dot(resid, proj[:, c * width:(c + 1) * width], preferred_element_type=F32)
        for d in range(half):
            s1[c, d] = part[(2 * d + 1) * span:(2 * d + 2) * span].astype(BF16)
            g0[c, d] = part[2 * d * span:(2 * d + 1) * span]
        rs1.append(send(s1.at[c], r1.at[c], rs1_s.at[c], rs1_r.at[c], pair))
    rs2 = [[None] * half for c in range(CHUNKS)]
    for c in range(CHUNKS):
        rs1[c].wait_recv()
        for d in range(1, half):
            s2[c, d - 1] = (g0[c, d] + r1[c, d].astype(F32)).astype(BF16)
            rs2[c][d] = send(s2.at[c, d - 1], r2.at[c, half - d - 1], rs2_s.at[c, d - 1],
                             rs2_r.at[c, half - d - 1], peers[d])
        g0[c, 0] = g0[c, 0] + r1[c, 0].astype(F32)
    rs3 = [[None] * views for c in range(CHUNKS)]
    for c in range(CHUNKS):
        total = g0[c, 0]
        for d in range(1, half):
            rs2[c][half - d].wait_recv()
            total = total + r2[c, d - 1].astype(F32)
        r3[c, v] = total.astype(BF16)
        for d in range(1, views):
            rs3[c][d] = send(r3.at[c, v], r3.at[c, v], rs3_s.at[c, d - 1], rs3_r.at[c, views - d - 1], others[d])
    for c in range(CHUNKS):
        cols = slice(c * width, (c + 1) * width)
        for d in range(1, views):
            source = lax.rem(v + views - d, views)
            pltpu.make_async_remote_copy(r3.at[c, source], r3.at[c, source], rs3_s.at[c, d - 1],
                                         rs3_r.at[c, views - d - 1], device_id=others[d],
                                         device_id_type=MESH).wait_recv()
        grad = r3[c, 0].astype(F32)
        for w in range(1, views):
            grad = grad + r3[c, w].astype(F32)
        grad = grad * float(views_all) ** (-0.5)
        for m in range(mat_count):
            total = nw[m, 0, :, cols].astype(F32) * grad[:depth]
            for k in range(1, mat_count):
                total = total + nw[m, k, :, cols].astype(F32) * grad[k * depth:(k + 1) * depth]
            out[m, :, cols] = base[m, :, cols] - total

    @pl.when(jnp.logical_not(first))
    def _():
        to_below.wait_send()

    @pl.when(jnp.logical_not(last))
    def _():
        to_above.wait_send()

    for c in range(CHUNKS):
        agp[c].wait_send()
        rs1[c].wait_send()
        for d in range(1, half):
            agy[c][d].wait_send()
            agf[c][d].wait_send()
            rs2[c][d].wait_send()
        for d in range(1, views):
            rs3[c][d].wait_send()


def body(volume, projector, counts, atten, newton):
    views, rows, mats = (lax.axis_size(a) for a in ("view", "row", "mat"))
    depth, mat_count, pixels = volume.shape
    columns = projector.shape[1]
    bins = atten.shape[0]
    views_all = projector.shape[0] * views * mats
    width = pixels // CHUNKS
    half = mats // 2
    span = depth * mat_count
    vol_t = jnp.transpose(volume, (1, 0, 2))
    cnt = counts.reshape(mats, depth, bins, columns)
    nw_t = jnp.transpose(newton, (1, 2, 0, 3))
    dims = (views, rows, mats, mat_count, bins, depth, width, views_all)
    hbm = pl.BlockSpec(memory_space=pltpu.HBM)
    dma = pltpu.SemaphoreType.DMA
    out = pl.pallas_call(
        functools.partial(kernel, dims),
        out_shape=jax.ShapeDtypeStruct((mat_count, depth, pixels), F32),
        in_specs=[hbm] * 5,
        out_specs=pl.BlockSpec(memory_space=pltpu.VMEM),
        scratch_shapes=[
            pltpu.VMEM((mat_count, depth, pixels), F32),
            pltpu.VMEM((columns, pixels), BF16),
            pltpu.VMEM((mats, depth, bins, columns), BF16),
            pltpu.VMEM((mats, bins, depth, columns), F32),
            pltpu.VMEM((mat_count, mat_count, depth, pixels), BF16),
            pltpu.SMEM(atten.shape, F32),
            pltpu.VMEM((2, mat_count, pixels), F32),
            pltpu.VMEM((2, mat_count, pixels), F32),
            pltpu.VMEM((CHUNKS, mats, span, width), BF16),
            pltpu.VMEM((mats * span, columns), F32),
            pltpu.VMEM((mats, span, columns), BF16),
            pltpu.VMEM((mat_count, depth, pixels), F32),
            pltpu.VMEM((CHUNKS, half, span, width), F32),
            pltpu.VMEM((CHUNKS, half, span, width), BF16),
            pltpu.VMEM((CHUNKS, half, span, width), BF16),
            pltpu.VMEM((CHUNKS, half - 1, span, width), BF16),
            pltpu.VMEM((CHUNKS, half - 1, span, width), BF16),
            pltpu.VMEM((CHUNKS, views, span, width), BF16),
            dma((4,)), dma((CHUNKS,)), dma((CHUNKS,)), dma((2,)), dma((2,)),
            dma((CHUNKS,)), dma((CHUNKS,)),
            dma((CHUNKS, half - 1)), dma((CHUNKS, half - 1)),
            dma((CHUNKS, half - 1)), dma((CHUNKS, half - 1)),
            dma((CHUNKS,)), dma((CHUNKS,)),
            dma((CHUNKS, half - 1)), dma((CHUNKS, half - 1)),
            dma((CHUNKS, views - 1)), dma((CHUNKS, views - 1)),
        ],
        compiler_params=pltpu.CompilerParams(
            collective_id=0, has_side_effects=True, vmem_limit_bytes=67043328 - ROOM
        ),
    )(vol_t, projector, cnt, nw_t, atten)
    return jnp.transpose(out, (1, 0, 2))


def solution(mesh):
    in_specs = (
        P(("row", "mat"), None, None),
        P(("view", "mat"), None, None),
        P(("view", "mat"), "row", None, None),
        P(),
        P(("row", "mat"), None, None, None),
    )
    out_specs = P(("row", "mat"), None, None)
    return jax.shard_map(body, mesh=mesh, in_specs=in_specs, out_specs=out_specs, check_vma=False)
```

```python
import functools

import jax
import jax.numpy as jnp
from jax import lax
from jax.experimental import pallas as pl
from jax.experimental.pallas import tpu as pltpu
from jax.sharding import PartitionSpec as P

PX = 1024
CHUNKS = 4
PARTS = 4
ROOM = 208 * 1024
MESH = pl.DeviceIdType.MESH
F32 = jnp.float32
BF16 = jnp.bfloat16


def shift_rows(field, by):
    zero = jnp.zeros((field.shape[0], PX), F32)
    if by > 0:
        return jnp.concatenate([zero, field[:, :-PX]], 1)
    return jnp.concatenate([field[:, PX:], zero], 1)


def shift_pix(field, by):
    size = field.shape[1]
    column = lax.broadcasted_iota(jnp.int32, field.shape, 1) % PX
    rolled = pltpu.roll(field, by % size, 1)
    edge = 0 if by > 0 else PX - 1
    return jnp.where(column == edge, 0.0, rolled)


def kernel(dims, vt_hbm, proj_hbm, cnt_hbm, nw_hbm, atten_hbm, out,
           vt, proj, cnt_in, cnt, nw, atten, edge, halo, xs, acc, res, base, g0, s1, r1, s2, r2, r3,
           loc_sem, vol_sem, proj_sem, halo_s, halo_r, agp_s, agp_r, agy_s, agy_r, agf_s, agf_r,
           rs1_s, rs1_r, rs2_s, rs2_r, rs3_s, rs3_r):
    views, rows, mats, mat_count, bins, depth, width, piece, views_all = dims
    half = mats // 2
    v, r, i = lax.axis_index("view"), lax.axis_index("row"), lax.axis_index("mat")
    par = i % 2
    group = i // 2
    pair = (v, r, i + 1 - 2 * par)
    peers = [None] + [(v, r, 2 * lax.rem(group + d, half) + par) for d in range(1, half)]
    others = [None] + [(lax.rem(v + d, views), r, i) for d in range(1, views)]
    slab = r * mats + i
    slabs = rows * mats
    up, down = lax.rem(slab + 1, slabs), lax.rem(slab + slabs - 1, slabs)
    above = (v, up // mats, up % mats)
    below = (v, down // mats, down % mats)

    barrier = pltpu.get_barrier_semaphore()
    last, first = slab == slabs - 1, slab == 0
    greet = [pair] + peers[1:] + others[1:]
    for device in greet:
        pl.semaphore_signal(barrier, inc=1, device_id=device, device_id_type=MESH)

    @pl.when(jnp.logical_not(first))
    def _():
        pl.semaphore_signal(barrier, inc=1, device_id=below, device_id_type=MESH)

    @pl.when(jnp.logical_not(last))
    def _():
        pl.semaphore_signal(barrier, inc=1, device_id=above, device_id_type=MESH)

    load_vol = []
    for c in range(CHUNKS):
        cols = pl.ds(c * width, width)
        load_vol.append(pltpu.make_async_copy(vt_hbm.at[:, :, cols], vt.at[:, :, cols], vol_sem.at[c]))
        load_vol[c].start()
    load_proj = []
    for c in range(CHUNKS):
        cols = pl.ds(c * width, width)
        load_proj.append(pltpu.make_async_copy(proj_hbm.at[0, :, cols], proj.at[:, cols], proj_sem.at[c]))
        load_proj[c].start()
    load_cnt = pltpu.make_async_copy(cnt_hbm, cnt_in, loc_sem.at[1])
    load_att = pltpu.make_async_copy(atten_hbm, atten, loc_sem.at[3])
    load_att.start()
    load_cnt.start()
    load_nw = pltpu.make_async_copy(nw_hbm, nw, loc_sem.at[2])
    load_nw.start()

    def send(src, dst, s, t, device):
        copy = pltpu.make_async_remote_copy(src, dst, s, t, device_id=device, device_id_type=MESH)
        copy.start()
        return copy

    def halo_copy(way, device):
        return pltpu.make_async_remote_copy(edge.at[way], halo.at[way], halo_s.at[way], halo_r.at[way],
                                            device_id=device, device_id_type=MESH)

    to_below, to_above = halo_copy(0, below), halo_copy(1, above)
    agy = [[None] * half for c in range(CHUNKS)]
    agp = []
    for c in range(CHUNKS):
        cols = slice(c * width, (c + 1) * width)
        if c == 0:
            load_vol[c].wait()
        xs[c, 0] = jnp.concatenate([vt[m, :, cols] for m in range(mat_count)], 0).astype(BF16)
        if c == 0:
            ends = jnp.where(first, 1, 0) + jnp.where(last, 1, 0)
            pl.semaphore_wait(barrier, len(greet) + 2 - ends)
        for d in range(1, half):
            agy[c][d] = send(xs.at[c, 0], xs.at[c, 2 * (half - d)], agy_s.at[c, d - 1],
                             agy_r.at[c, half - d - 1], peers[d])
        agp.append(send(xs.at[c, 0], xs.at[c, 1], agp_s.at[c], agp_r.at[c], pair))
        if c == 0:
            for rest in load_vol[1:]:
                rest.wait()
            edge[0] = jnp.concatenate([vt[m, 0:1, :] for m in range(mat_count)], 0)
            edge[1] = jnp.concatenate([vt[m, depth - 1:depth, :] for m in range(mat_count)], 0)

            @pl.when(jnp.logical_not(first))
            def _():
                to_below.start()

            @pl.when(jnp.logical_not(last))
            def _():
                to_above.start()

    load_att.wait()
    load_cnt.wait()
    for j in range(mats):
        tiles = [cnt_in[j, a].astype(F32) for a in range(depth)]
        for b in range(bins):
            cnt[j, b] = jnp.concatenate([tile[b:b + 1] for tile in tiles], 0)

    def regularise():
        @pl.when(jnp.logical_not(last))
        def _():
            to_below.wait_recv()

        @pl.when(last)
        def _():
            halo[0] = jnp.zeros(halo.shape[1:], F32)

        @pl.when(jnp.logical_not(first))
        def _():
            to_above.wait_recv()

        @pl.when(first)
        def _():
            halo[1] = jnp.zeros(halo.shape[1:], F32)

        load_nw.wait()
        z = lax.broadcasted_iota(jnp.int32, vt.shape[1:], 0)
        cur = [vt[m] for m in range(mat_count)]
        after = [jnp.where(z == depth - 1, halo[0, m:m + 1, :], pltpu.roll(cur[m], depth - 1, 0))
                 for m in range(mat_count)]
        before = [jnp.where(z == 0, halo[1, m:m + 1, :], pltpu.roll(cur[m], 1, 0)) for m in range(mat_count)]

        def fluxes(lower, upper):
            dz = [b - a for a, b in zip(lower, upper)]
            dy = [shift_rows(a, -1) - a for a in lower]
            dx = [shift_pix(a, -1) - a for a in lower]
            total = 0.25
            for m in range(mat_count):
                total = total + (dz[m] * dz[m] + dy[m] * dy[m] + dx[m] * dx[m])
            scale = 1.0 / jnp.sqrt(total)
            return [a * scale for a in dz], [a * scale for a in dy], [a * scale for a in dx]

        qz, qy, qx = fluxes(cur, after)
        pz, _, _ = fluxes(before, cur)
        tv = []
        for m in range(mat_count):
            prev_z = jnp.where(jnp.logical_and(first, z == 0), 0.0, pz[m])
            tv.append(0.5 * ((prev_z - qz[m]) + (shift_rows(qy[m], 1) - qy[m]) + (shift_pix(qx[m], 1) - qx[m])))
        for m in range(mat_count):
            total = nw[m, 0].astype(F32) * tv[0]
            for k in range(1, mat_count):
                total = total + nw[m, k].astype(F32) * tv[k]
            base[m] = cur[m] - total

    agf = [[None] * half for c in range(CHUNKS)]

    def relay(c):
        for d in range(1, half):
            agy[c][half - d].wait_recv()
            agf[c][d] = send(xs.at[c, 2 * d], xs.at[c, 2 * d + 1], agf_s.at[c, d - 1], agf_r.at[c, d - 1], pair)

    def forward(c):
        load_proj[c].wait()
        agp[c].wait_recv()
        for d in range(1, half):
            agf[c][d].wait_recv()
        x = jnp.concatenate([xs[c, s] for s in range(mats)], 0)
        part = lax.dot_general(x, proj[:, c * width:(c + 1) * width], (((1,), (1,)), ((), ())),
                               preferred_element_type=F32)
        if c == 0:
            acc[...] = part
        else:
            acc[...] += part

    lag = CHUNKS // 2
    for c in range(CHUNKS):
        relay(c)
        if c == 0:
            regularise()
        if c >= lag:
            forward(c - lag)
    for c in range(CHUNKS - lag, CHUNKS):
        forward(c)

    span = mat_count * depth
    for s in range(mats):
        owner = 2 * lax.rem(group + s // 2, half) + (par if s % 2 == 0 else 1 - par)
        line = [acc[s * span + m * depth:s * span + (m + 1) * depth, :] for m in range(mat_count)]
        parts = [None] * mat_count
        for b in range(bins):
            expo = atten[b, 0] * line[0]
            for m in range(1, mat_count):
                expo = expo + atten[b, m] * line[m]
            diff = cnt[owner, b] - jnp.exp(-expo)
            for m in range(mat_count):
                term = atten[b, m] * diff
                parts[m] = term if parts[m] is None else parts[m] + term
        res[s] = jnp.concatenate(parts, 0).astype(BF16)

    rs1 = []
    resid = jnp.concatenate([res[s] for s in range(mats)], 0)
    for c in range(PARTS):
        part = jnp.dot(resid, proj[:, c * piece:(c + 1) * piece], preferred_element_type=F32)
        for d in range(half):
            s1[c, d] = part[(2 * d + 1) * span:(2 * d + 2) * span].astype(BF16)
            g0[c, d] = part[2 * d * span:(2 * d + 1) * span]
        rs1.append(send(s1.at[c], r1.at[c], rs1_s.at[c], rs1_r.at[c], pair))
    rs2 = [[None] * half for c in range(PARTS)]
    for c in range(PARTS):
        rs1[c].wait_recv()
        for d in range(1, half):
            s2[c, d - 1] = (g0[c, d] + r1[c, d].astype(F32)).astype(BF16)
            rs2[c][d] = send(s2.at[c, d - 1], r2.at[c, half - d - 1], rs2_s.at[c, d - 1],
                             rs2_r.at[c, half - d - 1], peers[d])
        g0[c, 0] = g0[c, 0] + r1[c, 0].astype(F32)
    rs3 = [[None] * views for c in range(PARTS)]
    for c in range(PARTS):
        total = g0[c, 0]
        for d in range(1, half):
            rs2[c][half - d].wait_recv()
            total = total + r2[c, d - 1].astype(F32)
        r3[c, v] = total.astype(BF16)
        for d in range(1, views):
            rs3[c][d] = send(r3.at[c, v], r3.at[c, v], rs3_s.at[c, d - 1], rs3_r.at[c, views - d - 1], others[d])
    for c in range(PARTS):
        cols = slice(c * piece, (c + 1) * piece)
        for d in range(1, views):
            source = lax.rem(v + views - d, views)
            pltpu.make_async_remote_copy(r3.at[c, source], r3.at[c, source], rs3_s.at[c, d - 1],
                                         rs3_r.at[c, views - d - 1], device_id=others[d],
                                         device_id_type=MESH).wait_recv()
        grad = r3[c, 0].astype(F32)
        for w in range(1, views):
            grad = grad + r3[c, w].astype(F32)
        grad = grad * float(views_all) ** (-0.5)
        for m in range(mat_count):
            total = nw[m, 0, :, cols].astype(F32) * grad[:depth]
            for k in range(1, mat_count):
                total = total + nw[m, k, :, cols].astype(F32) * grad[k * depth:(k + 1) * depth]
            out[m, :, cols] = base[m, :, cols] - total

    @pl.when(jnp.logical_not(first))
    def _():
        to_below.wait_send()

    @pl.when(jnp.logical_not(last))
    def _():
        to_above.wait_send()

    for c in range(CHUNKS):
        agp[c].wait_send()
        for d in range(1, half):
            agy[c][d].wait_send()
            agf[c][d].wait_send()
    for c in range(PARTS):
        rs1[c].wait_send()
        for d in range(1, half):
            rs2[c][d].wait_send()
        for d in range(1, views):
            rs3[c][d].wait_send()


def body(volume, projector, counts, atten, newton):
    views, rows, mats = (lax.axis_size(a) for a in ("view", "row", "mat"))
    depth, mat_count, pixels = volume.shape
    columns = projector.shape[1]
    bins = atten.shape[0]
    views_all = projector.shape[0] * views * mats
    width = pixels // CHUNKS
    piece = pixels // PARTS
    half = mats // 2
    span = depth * mat_count
    vol_t = jnp.transpose(volume, (1, 0, 2))
    cnt = counts.reshape(mats, depth, bins, columns)
    nw_t = jnp.transpose(newton, (1, 2, 0, 3))
    dims = (views, rows, mats, mat_count, bins, depth, width, piece, views_all)
    hbm = pl.BlockSpec(memory_space=pltpu.HBM)
    dma = pltpu.SemaphoreType.DMA
    out = pl.pallas_call(
        functools.partial(kernel, dims),
        out_shape=pltpu.VMEM((mat_count, depth, pixels), F32),
        in_specs=[hbm] * 5,
        out_specs=pl.BlockSpec(memory_space=pltpu.VMEM),
        scratch_shapes=[
            pltpu.VMEM((mat_count, depth, pixels), F32),
            pltpu.VMEM((columns, pixels), BF16),
            pltpu.VMEM((mats, depth, bins, columns), BF16),
            pltpu.VMEM((mats, bins, depth, columns), F32),
            pltpu.VMEM((mat_count, mat_count, depth, pixels), BF16),
            pltpu.SMEM(atten.shape, F32),
            pltpu.VMEM((2, mat_count, pixels), F32),
            pltpu.VMEM((2, mat_count, pixels), F32),
            pltpu.VMEM((CHUNKS, mats, span, width), BF16),
            pltpu.VMEM((mats * span, columns), F32),
            pltpu.VMEM((mats, span, columns), BF16),
            pltpu.VMEM((mat_count, depth, pixels), F32),
            pltpu.VMEM((PARTS, half, span, piece), F32),
            pltpu.VMEM((PARTS, half, span, piece), BF16),
            pltpu.VMEM((PARTS, half, span, piece), BF16),
            pltpu.VMEM((PARTS, half - 1, span, piece), BF16),
            pltpu.VMEM((PARTS, half - 1, span, piece), BF16),
            pltpu.VMEM((PARTS, views, span, piece), BF16),
            dma((4,)), dma((CHUNKS,)), dma((CHUNKS,)), dma((2,)), dma((2,)),
            dma((CHUNKS,)), dma((CHUNKS,)),
            dma((CHUNKS, half - 1)), dma((CHUNKS, half - 1)),
            dma((CHUNKS, half - 1)), dma((CHUNKS, half - 1)),
            dma((PARTS,)), dma((PARTS,)),
            dma((PARTS, half - 1)), dma((PARTS, half - 1)),
            dma((PARTS, views - 1)), dma((PARTS, views - 1)),
        ],
        compiler_params=pltpu.CompilerParams(
            collective_id=0, has_side_effects=True, vmem_limit_bytes=67043328 - ROOM
        ),
    )(vol_t, projector, cnt, nw_t, atten)
    return jnp.transpose(out, (1, 0, 2))


def solution(mesh):
    in_specs = (
        P(("row", "mat"), None, None),
        P(("view", "mat"), None, None),
        P(("view", "mat"), "row", None, None),
        P(),
        P(("row", "mat"), None, None, None),
    )
    out_specs = P(("row", "mat"), None, None)
    return jax.shard_map(body, mesh=mesh, in_specs=in_specs, out_specs=out_specs, check_vma=False)
```

```python
import functools

import jax
import jax.numpy as jnp
from jax import lax
from jax.experimental import pallas as pl
from jax.experimental.pallas import tpu as pltpu
from jax.sharding import PartitionSpec as P

PX = 1024
CHUNKS = 4
PARTS = 4
BEHIND = 2
ROOM = 208 * 1024
MESH = pl.DeviceIdType.MESH
F32 = jnp.float32
BF16 = jnp.bfloat16


def shift_rows(field, by):
    zero = jnp.zeros((field.shape[0], PX), F32)
    if by > 0:
        return jnp.concatenate([zero, field[:, :-PX]], 1)
    return jnp.concatenate([field[:, PX:], zero], 1)


def shift_pix(field, by):
    size = field.shape[1]
    column = lax.broadcasted_iota(jnp.int32, field.shape, 1) % PX
    rolled = pltpu.roll(field, by % size, 1)
    edge = 0 if by > 0 else PX - 1
    return jnp.where(column == edge, 0.0, rolled)


def kernel(dims, vt_hbm, proj_hbm, cnt_hbm, nw_hbm, atten_hbm, out,
           vt, proj, cnt_in, cnt, nw, atten, edge, halo, xs, acc, res, base, g0, s1, r1, s2, r2, r3,
           loc_sem, vol_sem, proj_sem, halo_s, halo_r, agp_s, agp_r, agy_s, agy_r, agf_s, agf_r,
           rs1_s, rs1_r, rs2_s, rs2_r, rs3_s, rs3_r):
    views, rows, mats, mat_count, bins, depth, width, piece, views_all = dims
    half = mats // 2
    v, r, i = lax.axis_index("view"), lax.axis_index("row"), lax.axis_index("mat")
    par = i % 2
    group = i // 2
    pair = (v, r, i + 1 - 2 * par)
    peers = [None] + [(v, r, 2 * lax.rem(group + d, half) + par) for d in range(1, half)]
    others = [None] + [(lax.rem(v + d, views), r, i) for d in range(1, views)]
    slab = r * mats + i
    slabs = rows * mats
    up, down = lax.rem(slab + 1, slabs), lax.rem(slab + slabs - 1, slabs)
    above = (v, up // mats, up % mats)
    below = (v, down // mats, down % mats)

    barrier = pltpu.get_barrier_semaphore()
    last, first = slab == slabs - 1, slab == 0
    greet = [pair] + peers[1:] + others[1:]
    for device in greet:
        pl.semaphore_signal(barrier, inc=1, device_id=device, device_id_type=MESH)

    @pl.when(jnp.logical_not(first))
    def _():
        pl.semaphore_signal(barrier, inc=1, device_id=below, device_id_type=MESH)

    @pl.when(jnp.logical_not(last))
    def _():
        pl.semaphore_signal(barrier, inc=1, device_id=above, device_id_type=MESH)

    load_vol = []
    for c in range(CHUNKS):
        cols = pl.ds(c * width, width)
        load_vol.append(pltpu.make_async_copy(vt_hbm.at[:, :, cols], vt.at[:, :, cols], vol_sem.at[c]))
        load_vol[c].start()
    load_proj = []
    for c in range(CHUNKS):
        cols = pl.ds(c * width, width)
        load_proj.append(pltpu.make_async_copy(proj_hbm.at[0, :, cols], proj.at[:, cols], proj_sem.at[c]))
        load_proj[c].start()
    load_cnt = pltpu.make_async_copy(cnt_hbm, cnt_in, loc_sem.at[1])
    load_att = pltpu.make_async_copy(atten_hbm, atten, loc_sem.at[3])
    load_att.start()
    load_cnt.start()
    load_nw = pltpu.make_async_copy(nw_hbm, nw, loc_sem.at[2])
    load_nw.start()

    def send(src, dst, s, t, device):
        copy = pltpu.make_async_remote_copy(src, dst, s, t, device_id=device, device_id_type=MESH)
        copy.start()
        return copy

    def halo_copy(way, device):
        return pltpu.make_async_remote_copy(edge.at[way], halo.at[way], halo_s.at[way], halo_r.at[way],
                                            device_id=device, device_id_type=MESH)

    to_below, to_above = halo_copy(0, below), halo_copy(1, above)
    agy = [[None] * half for c in range(CHUNKS)]
    agp = []
    for c in range(CHUNKS):
        cols = slice(c * width, (c + 1) * width)
        load_vol[c].wait()
        xs[c, 0] = jnp.concatenate([vt[m, :, cols] for m in range(mat_count)], 0).astype(BF16)
        if c == 0:
            ends = jnp.where(first, 1, 0) + jnp.where(last, 1, 0)
            pl.semaphore_wait(barrier, len(greet) + 2 - ends)
        for d in range(1, half):
            agy[c][d] = send(xs.at[c, 0], xs.at[c, 2 * (half - d)], agy_s.at[c, d - 1],
                             agy_r.at[c, half - d - 1], peers[d])
        agp.append(send(xs.at[c, 0], xs.at[c, 1], agp_s.at[c], agp_r.at[c], pair))
    edge[0] = jnp.concatenate([vt[m, 0:1, :] for m in range(mat_count)], 0)
    edge[1] = jnp.concatenate([vt[m, depth - 1:depth, :] for m in range(mat_count)], 0)

    @pl.when(jnp.logical_not(first))
    def _():
        to_below.start()

    @pl.when(jnp.logical_not(last))
    def _():
        to_above.start()

    load_att.wait()
    load_cnt.wait()
    for j in range(mats):
        tiles = [cnt_in[j, a].astype(F32) for a in range(depth)]
        for b in range(bins):
            cnt[j, b] = jnp.concatenate([tile[b:b + 1] for tile in tiles], 0)

    def regularise():
        @pl.when(jnp.logical_not(last))
        def _():
            to_below.wait_recv()

        @pl.when(last)
        def _():
            halo[0] = jnp.zeros(halo.shape[1:], F32)

        @pl.when(jnp.logical_not(first))
        def _():
            to_above.wait_recv()

        @pl.when(first)
        def _():
            halo[1] = jnp.zeros(halo.shape[1:], F32)

        load_nw.wait()
        z = lax.broadcasted_iota(jnp.int32, vt.shape[1:], 0)
        cur = [vt[m] for m in range(mat_count)]
        after = [jnp.where(z == depth - 1, halo[0, m:m + 1, :], pltpu.roll(cur[m], depth - 1, 0))
                 for m in range(mat_count)]
        before = [jnp.where(z == 0, halo[1, m:m + 1, :], pltpu.roll(cur[m], 1, 0)) for m in range(mat_count)]

        def fluxes(lower, upper):
            dz = [b - a for a, b in zip(lower, upper)]
            dy = [shift_rows(a, -1) - a for a in lower]
            dx = [shift_pix(a, -1) - a for a in lower]
            total = 0.25
            for m in range(mat_count):
                total = total + (dz[m] * dz[m] + dy[m] * dy[m] + dx[m] * dx[m])
            scale = 1.0 / jnp.sqrt(total)
            return [a * scale for a in dz], [a * scale for a in dy], [a * scale for a in dx]

        qz, qy, qx = fluxes(cur, after)
        pz, _, _ = fluxes(before, cur)
        tv = []
        for m in range(mat_count):
            prev_z = jnp.where(jnp.logical_and(first, z == 0), 0.0, pz[m])
            tv.append(0.5 * ((prev_z - qz[m]) + (shift_rows(qy[m], 1) - qy[m]) + (shift_pix(qx[m], 1) - qx[m])))
        for m in range(mat_count):
            total = nw[m, 0].astype(F32) * tv[0]
            for k in range(1, mat_count):
                total = total + nw[m, k].astype(F32) * tv[k]
            base[m] = cur[m] - total

    agf = [[None] * half for c in range(CHUNKS)]

    def relay(c):
        for d in range(1, half):
            agy[c][half - d].wait_recv()
            agf[c][d] = send(xs.at[c, 2 * d], xs.at[c, 2 * d + 1], agf_s.at[c, d - 1], agf_r.at[c, d - 1], pair)

    def forward(c):
        load_proj[c].wait()
        agp[c].wait_recv()
        for d in range(1, half):
            agf[c][d].wait_recv()
        x = jnp.concatenate([xs[c, s] for s in range(mats)], 0)
        part = lax.dot_general(x, proj[:, c * width:(c + 1) * width], (((1,), (1,)), ((), ())),
                               preferred_element_type=F32)
        if c == 0:
            acc[...] = part
        else:
            acc[...] += part

    lag = CHUNKS // 2
    for c in range(CHUNKS):
        relay(c)
        if c >= lag:
            forward(c - lag)
    for c in range(CHUNKS - lag, CHUNKS):
        forward(c)

    span = mat_count * depth
    for s in range(mats):
        owner = 2 * lax.rem(group + s // 2, half) + (par if s % 2 == 0 else 1 - par)
        line = [acc[s * span + m * depth:s * span + (m + 1) * depth, :] for m in range(mat_count)]
        parts = [None] * mat_count
        for b in range(bins):
            expo = atten[b, 0] * line[0]
            for m in range(1, mat_count):
                expo = expo + atten[b, m] * line[m]
            diff = cnt[owner, b] - jnp.exp(-expo)
            for m in range(mat_count):
                term = atten[b, m] * diff
                parts[m] = term if parts[m] is None else parts[m] + term
        res[s] = jnp.concatenate(parts, 0).astype(BF16)

    rs1 = [[None] * half for c in range(PARTS)]

    def swap(c, d):
        rs1[c][d] = send(s1.at[c, d], r1.at[c, d], rs1_s.at[c, d], rs1_r.at[c, d], pair)

    rs2 = [[None] * half for c in range(PARTS)]

    def across(c):
        for d in range(1, half):
            rs1[c][d].wait_recv()
            s2[c, d - 1] = (g0[c, d] + r1[c, d].astype(F32)).astype(BF16)
            rs2[c][d] = send(s2.at[c, d - 1], r2.at[c, half - d - 1], rs2_s.at[c, d - 1],
                             rs2_r.at[c, half - d - 1], peers[d])

    resid = jnp.concatenate([res[s] for s in range(mats)], 0)
    for c in range(PARTS):
        part = jnp.dot(resid, proj[:, c * piece:(c + 1) * piece], preferred_element_type=F32)
        for d in range(half):
            s1[c, d] = part[(2 * d + 1) * span:(2 * d + 2) * span].astype(BF16)
            g0[c, d] = part[2 * d * span:(2 * d + 1) * span]
        for d in range(1, half):
            swap(c, d)
        if c >= BEHIND:
            across(c - BEHIND)
    for c in range(PARTS - BEHIND, PARTS):
        across(c)
    for c in range(PARTS):
        swap(c, 0)
    regularise()
    rs3 = [[None] * views for c in range(PARTS)]
    for c in range(PARTS):
        rs1[c][0].wait_recv()
        total = g0[c, 0] + r1[c, 0].astype(F32)
        for d in range(1, half):
            rs2[c][half - d].wait_recv()
            total = total + r2[c, d - 1].astype(F32)
        r3[c, v] = total.astype(BF16)
        for d in range(1, views):
            rs3[c][d] = send(r3.at[c, v], r3.at[c, v], rs3_s.at[c, d - 1], rs3_r.at[c, views - d - 1], others[d])
    for c in range(PARTS):
        cols = slice(c * piece, (c + 1) * piece)
        for d in range(1, views):
            source = lax.rem(v + views - d, views)
            pltpu.make_async_remote_copy(r3.at[c, source], r3.at[c, source], rs3_s.at[c, d - 1],
                                         rs3_r.at[c, views - d - 1], device_id=others[d],
                                         device_id_type=MESH).wait_recv()
        grad = r3[c, 0].astype(F32)
        for w in range(1, views):
            grad = grad + r3[c, w].astype(F32)
        grad = grad * float(views_all) ** (-0.5)
        for m in range(mat_count):
            total = nw[m, 0, :, cols].astype(F32) * grad[:depth]
            for k in range(1, mat_count):
                total = total + nw[m, k, :, cols].astype(F32) * grad[k * depth:(k + 1) * depth]
            out[m, :, cols] = base[m, :, cols] - total

    @pl.when(jnp.logical_not(first))
    def _():
        to_below.wait_send()

    @pl.when(jnp.logical_not(last))
    def _():
        to_above.wait_send()

    for c in range(CHUNKS):
        agp[c].wait_send()
        for d in range(1, half):
            agy[c][d].wait_send()
            agf[c][d].wait_send()
    for c in range(PARTS):
        rs1[c][0].wait_send()
        for d in range(1, half):
            rs1[c][d].wait_send()
            rs2[c][d].wait_send()
        for d in range(1, views):
            rs3[c][d].wait_send()


def body(volume, projector, counts, atten, newton):
    views, rows, mats = (lax.axis_size(a) for a in ("view", "row", "mat"))
    depth, mat_count, pixels = volume.shape
    columns = projector.shape[1]
    bins = atten.shape[0]
    views_all = projector.shape[0] * views * mats
    width = pixels // CHUNKS
    piece = pixels // PARTS
    half = mats // 2
    span = depth * mat_count
    vol_t = jnp.transpose(volume, (1, 0, 2))
    cnt = counts.reshape(mats, depth, bins, columns)
    nw_t = jnp.transpose(newton, (1, 2, 0, 3))
    dims = (views, rows, mats, mat_count, bins, depth, width, piece, views_all)
    hbm = pl.BlockSpec(memory_space=pltpu.HBM)
    dma = pltpu.SemaphoreType.DMA
    out = pl.pallas_call(
        functools.partial(kernel, dims),
        out_shape=pltpu.VMEM((mat_count, depth, pixels), F32),
        in_specs=[hbm] * 5,
        out_specs=pl.BlockSpec(memory_space=pltpu.VMEM),
        scratch_shapes=[
            pltpu.VMEM((mat_count, depth, pixels), F32),
            pltpu.VMEM((columns, pixels), BF16),
            pltpu.VMEM((mats, depth, bins, columns), BF16),
            pltpu.VMEM((mats, bins, depth, columns), F32),
            pltpu.VMEM((mat_count, mat_count, depth, pixels), BF16),
            pltpu.SMEM(atten.shape, F32),
            pltpu.VMEM((2, mat_count, pixels), F32),
            pltpu.VMEM((2, mat_count, pixels), F32),
            pltpu.VMEM((CHUNKS, mats, span, width), BF16),
            pltpu.VMEM((mats * span, columns), F32),
            pltpu.VMEM((mats, span, columns), BF16),
            pltpu.VMEM((mat_count, depth, pixels), F32),
            pltpu.VMEM((PARTS, half, span, piece), F32),
            pltpu.VMEM((PARTS, half, span, piece), BF16),
            pltpu.VMEM((PARTS, half, span, piece), BF16),
            pltpu.VMEM((PARTS, half - 1, span, piece), BF16),
            pltpu.VMEM((PARTS, half - 1, span, piece), BF16),
            pltpu.VMEM((PARTS, views, span, piece), BF16),
            dma((4,)), dma((CHUNKS,)), dma((CHUNKS,)), dma((2,)), dma((2,)),
            dma((CHUNKS,)), dma((CHUNKS,)),
            dma((CHUNKS, half - 1)), dma((CHUNKS, half - 1)),
            dma((CHUNKS, half - 1)), dma((CHUNKS, half - 1)),
            dma((PARTS, half)), dma((PARTS, half)),
            dma((PARTS, half - 1)), dma((PARTS, half - 1)),
            dma((PARTS, views - 1)), dma((PARTS, views - 1)),
        ],
        compiler_params=pltpu.CompilerParams(
            collective_id=0, has_side_effects=True, vmem_limit_bytes=67043328 - ROOM
        ),
    )(vol_t, projector, cnt, nw_t, atten)
    return jnp.transpose(out, (1, 0, 2))


def solution(mesh):
    in_specs = (
        P(("row", "mat"), None, None),
        P(("view", "mat"), None, None),
        P(("view", "mat"), "row", None, None),
        P(),
        P(("row", "mat"), None, None, None),
    )
    out_specs = P(("row", "mat"), None, None)
    return jax.shard_map(body, mesh=mesh, in_specs=in_specs, out_specs=out_specs, check_vma=False)
```
